256 devices in a mesh: pix: 8 (over z), ang: 32 (over y, x, core).
Axes of the slice: x: 4, y: 4, z: 8, core: 2. Of those that a mesh axis runs over, the one named last changes fastest.
Arguments:
- volume: float32 [256, 128, 128], P(('pix', 'ang')), may hold values from -6 to 6
- projector: float32 [40960, 128, 128], P(('pix', 'ang')), may hold values from -0.078125 to 0.078125
- tile_ids: int32 [40960], P(('pix', 'ang')), may hold values from 0 to 1023, as said below
- counts: int32 [1024, 128, 128], P('ang'), may hold values from 64 to 4095
- ray_counts: int32 [32, 8], P('ang'), may hold values from 1 to 4, 20 in all within a row
Outputs:
- updated: float32 [256, 128, 128], P(('pix', 'ang'))
The draws below stay inside these ranges and needn't reach their ends.
Inputs may be any that keep to these rules, and one draw needn't show every extreme that they name: `tile_ids`: within each device's aligned block of 160 entries the values are distinct; value v names ray block v // 32 and pixel tile v % 32 of that device. `ray_counts`: each row sums to 20; the largest entry of every row is 4.
All inputs are finite; a program needn't handle non-finite values.
Results may differ from the reference program's by a relative error of at most 0.0001.
Values sent between devices are 32-bit elements; how exact they have to be, the bound alone decides.
A program may use at most 128 MiB of HBM per device.

```python
import math
import jax
import jax.numpy as jnp
import numpy as np
from jax import lax

TILE = 128
SL = 128
PT = 32
MOST = 4
K = 160
RB = 32
LIVE = 20
TILES_ALL = 40960
VOXEL_TILES = 256
RAY_ROWS = 1024
N_PIX = 8
N_ANG = 32


def draw_tile_ids(key, part):
    device_keys = jax.random.split(key, N_PIX * N_ANG)
    chosen = jax.vmap(lambda device_key: jax.random.permutation(device_key, RB * PT)[:K])(device_keys)
    return chosen.reshape(-1).astype(jnp.int32)


def place_ends(array, own_key, smallest, largest):
    longest = array.shape.index(max(array.shape))
    spots = []
    for shift in (0, 1):
        where = [jax.random.randint(jax.random.fold_in(own_key, axis), (), 0, length) for axis, length in enumerate(array.shape)]
        where[longest] = (where[longest] + shift) % array.shape[longest]
        spots.append(tuple(where))
    return array.at[spots[0]].set(smallest).at[spots[1]].set(largest)


def shard_levels(key, shape, pieces, smallest, high):
    factor_of = 1.0
    for dim, parts in pieces:
        heights = jax.random.uniform(jax.random.fold_in(jax.random.fold_in(key, 6), dim), (parts,), jnp.float32, smallest / len(pieces), high / len(pieces))
        factor_of = factor_of * jnp.repeat(jnp.exp(heights), shape[dim] // parts).reshape((-1,) + (1,) * (len(shape) - 1 - dim))
    return factor_of


def length_profile(number_of, total, most, skew):
    portions = [(1 << 20) // math.isqrt(standing ** skew) + 1 for standing in range(2, number_of + 1)]
    rest, holding = total - most - (number_of - 1), [1] * (number_of - 1)
    while rest > 0:
        free = [i for i in range(number_of - 1) if holding[i] < most]
        mass, remaining = sum([portions[i] for i in free]), rest
        for i in free:
            more = min(most - holding[i], max(1, remaining * portions[i] // mass), rest)
            holding[i] = holding[i] + more
            rest = rest - more
    return np.array([most] + holding)


def ragged_sizes(own_key, number_of, total, bound, skew):
    if number_of == 2:
        one = jax.random.randint(own_key, (), max(1, total - bound), min(bound, total - 1) + 1)
        return jnp.stack([one, total - one])
    tallies = jnp.asarray(length_profile(number_of, total, bound, skew), jnp.int32)
    pairs = (number_of - 1) // 2
    source_of, receiver = tallies[1:1 + 2 * pairs:2], tallies[2:2 + 2 * pairs:2]
    slack = jnp.minimum(source_of - 1, bound - receiver)
    shifted = jax.random.randint(jax.random.fold_in(own_key, 1), (pairs,), 0, 1 << 20) % (slack + 1)
    tallies = tallies.at[1:1 + 2 * pairs:2].set(source_of - shifted).at[2:2 + 2 * pairs:2].set(receiver + shifted)
    return tallies[jax.random.permutation(jax.random.fold_in(own_key, 2), number_of)]


def centred(rng, dims, spread, bound, cuts=(), kind=jnp.bfloat16):
    result = spread * jax.random.normal(rng, dims, jnp.float32)
    if cuts:
        result = result * shard_levels(rng, dims, cuts, -0.22, 0.18)
    return jnp.clip(result, -bound, bound).astype(kind)


def setup_inputs(seed: int = 0) -> dict:
    seeds = jax.random.split(jax.random.key(seed), 6)
    volume = centred(seeds[0], (VOXEL_TILES, SL, TILE), 1.0, 6.0, ((0, 256),), jnp.float32)
    projector = centred(seeds[1], (TILES_ALL, TILE, TILE), (TILE * K // MOST) ** -0.5, 0.078125, ((0, 256),), jnp.float32)
    tile_ids = draw_tile_ids(jax.random.fold_in(seeds[5], 71), 0)
    counts = place_ends(jax.random.randint(seeds[3], (RAY_ROWS, SL, TILE), 64, 4096), jax.random.fold_in(seeds[3], 1), 64, 4095).astype(jnp.int32)
    ray_counts = jax.vmap(lambda own: ragged_sizes(own, N_PIX, LIVE, MOST, 2))(jax.random.split(seeds[4], N_ANG)).reshape((N_ANG, N_PIX)).astype(jnp.int32)
    return dict(volume=volume, projector=projector, tile_ids=tile_ids, counts=counts, ray_counts=ray_counts)


blank_flux = 4096.0
step_size = 0.5


def reference(volume, projector, tile_ids, counts, ray_counts):
    highest = lax.Precision.HIGHEST
    device_total = N_PIX * N_ANG
    device_ids = jnp.arange(device_total, dtype=jnp.int32)
    pix_owner = device_ids // N_ANG
    angle_group = device_ids % N_ANG
    local_ids = tile_ids.reshape(device_total, K)
    ray_rows = (angle_group[:, None] * RB + local_ids // PT).astype(jnp.int32)
    pixel_cols = (pix_owner[:, None] * PT + local_ids % PT).astype(jnp.int32)
    blocks_all = projector.reshape(device_total, K, TILE, TILE)

    def forward(running, inputs):
        blocks, row_index, col_index = inputs
        picked = jnp.take(volume, col_index, axis=0)
        product = jnp.einsum("ksq,krq->ksr", picked, blocks, precision=highest)
        return running.at[row_index].add(product), None

    projected = lax.scan(forward, jnp.zeros((N_ANG * RB, SL, TILE), jnp.float32), (blocks_all, ray_rows, pixel_cols))[0]
    slot_index = jnp.arange(RB, dtype=jnp.int32)
    live_mask = (slot_index % MOST)[None, :] < ray_counts[:, slot_index // MOST]
    live_mask = live_mask.reshape(N_ANG * RB)[:, None, None]
    measured = counts.astype(jnp.float32)
    weights = jnp.where(live_mask, measured / blank_flux, 0.0)
    measured_data = jnp.where(live_mask, jnp.log(blank_flux / measured), 0.0)
    residual = weights * (projected - measured_data)

    def backward(running, inputs):
        blocks, row_index, col_index = inputs
        picked = jnp.take(residual, row_index, axis=0)
        product = jnp.einsum("ksr,krq->ksq", picked, blocks, precision=highest)
        return running.at[col_index].add(product), None

    gradient = lax.scan(backward, jnp.zeros((N_PIX * PT, SL, TILE), jnp.float32), (blocks_all, ray_rows, pixel_cols))[0]
    return volume - step_size * gradient
```

```python
import functools

import jax
import jax.numpy as jnp
from jax import lax
from jax.experimental import pallas as pl
from jax.experimental.pallas import tpu as pltpu
from jax.sharding import PartitionSpec as P

f32, bf16, i32 = jnp.float32, jnp.bfloat16, jnp.int32
BLANK = 4096.0
STEP = 0.5
NP, NY, NX, NC = 8, 4, 4, 2
MOST, LIVE = 4, 20
GROUP = 8
PIECES = 4
NT = (((1,), (1,)), ((), ()))
NN = (((1,), (0,)), ((), ()))
VMEM = pl.BlockSpec(memory_space=pltpu.VMEM)
SMEM = pl.BlockSpec(memory_space=pltpu.SMEM)
ANY = pl.BlockSpec(memory_space=pl.ANY)
MESH = pl.DeviceIdType.MESH


class Wires:
    def __init__(self, send, recv):
        self.send_sem, self.recv_sem, self.tags, self.started = send, recv, {}, []

    def copy(self, tag, src, dst, device):
        at = self.tags.setdefault(tag, len(self.tags))
        return pltpu.make_async_remote_copy(
            src_ref=src, dst_ref=dst, send_sem=self.send_sem.at[at], recv_sem=self.recv_sem.at[at],
            device_id=device, device_id_type=MESH,
        )

    def send(self, tag, src, dst, device):
        copy = self.copy(tag, src, dst, device)
        copy.start()
        self.started.append(copy)

    def wait(self, tag, dst, device):
        self.copy(tag, dst, dst, device).wait_recv()

    def drain(self):
        for copy in self.started:
            copy.wait_send()


def meet(devices):
    barrier = pltpu.get_barrier_semaphore()
    for device in devices:
        pl.semaphore_signal(barrier, inc=1, device_id=device, device_id_type=MESH)
    pl.semaphore_wait(barrier, len(devices))


def place():
    pix, ang = lax.axis_index("pix"), lax.axis_index("ang")
    core, x, y = lax.rem(ang, NC), lax.rem(ang // NC, NX), ang // (NC * NX)
    return pix, y, x, core


def ang_device(pix, y, x, core):
    return {"pix": pix, "ang": (y * NX + x) * NC + core}


def turn(i, by, n):
    return lax.rem(i + by + n, n)


def gather_kernel(vol, out, send, recv):
    pix, y, x, core = place()
    wires = Wires(send, recv)
    half = vol.shape[0] // 2
    quarter = half // 2
    partner = ang_device(pix, y, x, 1 - core)
    near = {
        ("x", 1): ang_device(pix, y, turn(x, 1, NX), core),
        ("x", -1): ang_device(pix, y, turn(x, -1, NX), core),
        ("y", 1): ang_device(pix, turn(y, 1, NY), x, core),
        ("y", -1): ang_device(pix, turn(y, -1, NY), x, core),
    }
    other = {"x": "y", "y": "x"}
    base = {"x": 0, "y": half}
    meet(list(near.values()) + [partner])

    def at(color, first, second, lo, n, c=core):
        dx, dy = (first, second) if color == "x" else (second, first)
        return out.at[turn(y, dy, NY), turn(x, dx, NX), c, pl.ds(base[color] + lo, n)]

    def spread(color, e, src=None):
        ref = at(color, e, 0, 0, half) if src is None else src
        for way in (1, -1):
            wires.send((color, 2, e, way), ref, at(color, e, 0, 0, half), near[other[color], way])
        wires.send((color, "p", e, 0), ref, at(color, e, 0, 0, half), partner)

    for color in ("x", "y"):
        src = vol.at[pl.ds(base[color], half)]
        for way in (1, -1):
            wires.send((color, 1, way), src, at(color, 0, 0, 0, half), near[color, way])
    for color in ("x", "y"):
        spread(color, 0, vol.at[pl.ds(base[color], half)])
    out[y, x, core] = vol[...]
    for way in (1, -1):
        for color in ("x", "y"):
            wires.wait((color, 1, way), at(color, -way, 0, 0, half), near[color, -way])
            lo = 0 if way == 1 else quarter
            part = at(color, -way, 0, lo, quarter)
            wires.send((color, 1.5, way), part, part, near[color, way])
            spread(color, -way)

    def second(e):
        for way in (1, -1):
            for color in ("x", "y"):
                ref = at(color, e, -way, 0, half)
                wires.wait((color, 2, e, way), ref, near[other[color], -way])
                lo = 0 if way == 1 else quarter
                part = at(color, e, -way, lo, quarter)
                wires.send((color, 2.5, e, way), part, part, near[other[color], way])
                wires.send((color, "p", e, -way), ref, ref, partner)

    second(0)
    for color in ("x", "y"):
        for way in (1, -1):
            lo = 0 if way == 1 else quarter
            wires.wait((color, 1.5, way), at(color, 2, 0, lo, quarter), near[color, -way])
        spread(color, 2)
    for e in (-1, 1, 2):
        second(e)
    for e in (0, -1, 1, 2):
        for color in ("x", "y"):
            for way in (1, -1):
                lo = 0 if way == 1 else quarter
                wires.wait((color, 2.5, e, way), at(color, e, 2, lo, quarter), near[other[color], -way])
            ref = at(color, e, 2, 0, half)
            wires.send((color, "p", e, 2), ref, ref, partner)
    for e in (0, -1, 1, 2):
        for f in (0, 1, -1, 2):
            for color in ("x", "y"):
                wires.wait((color, "p", e, f), at(color, e, f, 0, half, 1 - core), partner)
    wires.drain()


def gather_ang(vol):
    count = 2 * (2 + 2 + 8 + 8 + 16)
    shape = vol.shape[1:]
    return pl.pallas_call(
        gather_kernel,
        out_shape=jax.ShapeDtypeStruct((NY, NX, NC) + shape, f32),
        in_specs=[VMEM],
        out_specs=VMEM,
        scratch_shapes=[pltpu.SemaphoreType.DMA((count,)), pltpu.SemaphoreType.DMA((count,))],
        compiler_params=pltpu.CompilerParams(collective_id=0, has_side_effects=True),
        name="gather_ang",
    )(vol.reshape(shape)).reshape((NY * NX * NC,) + shape)


def scatter_kernel(grad, out, mine, far, near_in, mid, far2, near2, send, recv):
    pix, y, x, core = place()
    wires = Wires(send, recv)
    half = grad.shape[3] // 2
    quarter = half // 2
    partner = ang_device(pix, y, x, 1 - core)
    near = {
        ("x", 1): ang_device(pix, y, turn(x, 1, NX), core),
        ("x", -1): ang_device(pix, y, turn(x, -1, NX), core),
        ("y", 1): ang_device(pix, turn(y, 1, NY), x, core),
        ("y", -1): ang_device(pix, turn(y, -1, NY), x, core),
    }
    other = {"x": "y", "y": "x"}
    pos = {"x": x, "y": y}
    colors = (("x", 0, 0), ("y", 1, half))
    meet(list(near.values()) + [partner])

    def bundle(color, base, d, c):
        if color == "x":
            return grad.at[:, d, c, pl.ds(base, half)]
        return grad.at[d, :, c, pl.ds(base, half)]

    order = (2, 1, -1, 0)
    for d in order:
        for color, k, base in colors:
            at = turn(pos[color], d, 4)
            wires.send((color, "p", d), bundle(color, base, at, 1 - core), mine.at[k, at], partner)
    for d in order:
        for color, k, base in colors:
            at = turn(pos[color], d, 4)
            wires.wait((color, "p", d), mine.at[k, at], partner)
            mine[k, at] += bundle(color, base, at, core)[...]
            if d == 2:
                for w, way in enumerate((1, -1)):
                    rows = pl.ds(w * quarter, quarter)
                    wires.send((color, 1.5, way), mine.at[k, at, :, rows], far.at[k, w], near[color, way])
            elif d != 0:
                way = d
                w = 0 if way == 1 else 1
                rows = pl.ds((1 - w) * quarter, quarter)
                wires.send((color, 1, way, 0), mine.at[k, at, :, rows], near_in.at[k, w, :, rows], near[color, way])
    for w, way in enumerate((1, -1)):
        for color, k, base in colors:
            wires.wait((color, 1.5, way), far.at[k, w], near[color, -way])
            at = turn(pos[color], way, 4)
            rows = pl.ds(w * quarter, quarter)
            mine[k, at, :, rows] += far[k, w]
            wires.send((color, 1, way, 1), mine.at[k, at, :, rows], near_in.at[k, w, :, rows], near[color, way])
    for color, k, base in colors:
        at = pos[color]
        for w, way in enumerate((1, -1)):
            for part in (0, 1):
                rows = pl.ds(((1 - w) if part == 0 else w) * quarter, quarter)
                wires.wait((color, 1, way, part), near_in.at[k, w, :, rows], near[color, -way])
        mid[k] = mine[k, at] + (near_in[k, 0] + near_in[k, 1])
        second = other[color]
        at = turn(pos[second], 2, 4)
        for w, way in enumerate((1, -1)):
            rows = pl.ds(w * quarter, quarter)
            wires.send((color, 2.5, way), mid.at[k, at, rows], far2.at[k, w], near[second, way])
        for w, way in enumerate((1, -1)):
            at = turn(pos[second], way, 4)
            rows = pl.ds((1 - w) * quarter, quarter)
            wires.send((color, 2, way, 0), mid.at[k, at, rows], near2.at[k, w, rows], near[second, way])
    for w, way in enumerate((1, -1)):
        for color, k, base in colors:
            second = other[color]
            wires.wait((color, 2.5, way), far2.at[k, w], near[second, -way])
            at = turn(pos[second], way, 4)
            rows = pl.ds(w * quarter, quarter)
            mid[k, at, rows] += far2[k, w]
            wires.send((color, 2, way, 1), mid.at[k, at, rows], near2.at[k, w, rows], near[second, way])
    for color, k, base in colors:
        second = other[color]
        for w, way in enumerate((1, -1)):
            for part in (0, 1):
                rows = pl.ds(((1 - w) if part == 0 else w) * quarter, quarter)
                wires.wait((color, 2, way, part), near2.at[k, w, rows], near[second, -way])
        out[pl.ds(base, half)] = mid[k, pos[second]] + (near2[k, 0] + near2[k, 1])
    wires.drain()


def scatter_ang(grad):
    shape = grad.shape[1:]
    half, lanes = shape[0] // 2, shape[1]
    count = 2 * (4 + 2 + 4 + 2 + 4)
    return pl.pallas_call(
        scatter_kernel,
        out_shape=jax.ShapeDtypeStruct(shape, f32),
        in_specs=[VMEM],
        out_specs=VMEM,
        scratch_shapes=[
            pltpu.VMEM((2, 4, 4, half, lanes), f32),
            pltpu.VMEM((2, 2, 4, half // 2, lanes), f32),
            pltpu.VMEM((2, 2, 4, half, lanes), f32),
            pltpu.VMEM((2, 4, half, lanes), f32),
            pltpu.VMEM((2, 2, half // 2, lanes), f32),
            pltpu.VMEM((2, 2, half, lanes), f32),
            pltpu.SemaphoreType.DMA((count,)),
            pltpu.SemaphoreType.DMA((count,)),
        ],
        compiler_params=pltpu.CompilerParams(collective_id=1, has_side_effects=True),
        name="scatter_ang",
    )(grad.reshape((NY, NX, NC) + shape))


def exchange_kernel(part, weight, target, out, inbox, total, send, recv):
    me = lax.axis_index("pix")
    ang = lax.axis_index("ang")
    wires = Wires(send, recv)
    size = part.shape[1] // PIECES
    near = {way: {"pix": turn(me, way, NP), "ang": ang} for way in (1, -1)}
    meet(list(near.values()))

    def rows(i):
        return pl.ds(i * size, size)

    def goes_far(way, i):
        return (i < PIECES // 2) == (way == 1)

    order = {1: list(range(PIECES)), -1: list(range(PIECES // 2, PIECES)) + list(range(PIECES // 2))}
    pairs = [(way, order[way][n]) for n in range(PIECES) for way in (1, -1)]

    def box(way, d, i):
        return inbox.at[0 if way == 1 else 1, d - 1, rows(i)]

    def pass_on(way, d, i, src):
        wires.send(("r", way, d, i), src, box(way, d, i), near[way])

    for way, i in pairs:
        if goes_far(way, i):
            pass_on(way, 4, i, part.at[turn(me, 4, NP), rows(i)])
    for way, i in pairs:
        if not goes_far(way, i):
            pass_on(way, 3, i, part.at[turn(me, 3 * way, NP), rows(i)])
    for d in (3, 2, 1):
        for way, i in pairs:
            if d == 3 and not goes_far(way, i):
                continue
            wires.wait(("r", way, d + 1, i), box(way, d + 1, i), near[-way])
            w = 0 if way == 1 else 1
            inbox[w, d, rows(i)] += part[turn(me, d * way, NP), rows(i)]
            pass_on(way, d, i, inbox.at[w, d, rows(i)])

    def deliver(way, d, i):
        ref = out.at[turn(me, -d * way, NP), rows(i)]
        src = ref if d else total.at[rows(i)]
        wires.send(("g", way, d, i), src, ref, near[way])

    for i in range(PIECES):
        for way in (1, -1):
            wires.wait(("r", way, 1, i), box(way, 1, i), near[-way])
        summed = part[me, rows(i)] + (inbox[0, 0, rows(i)] + inbox[1, 0, rows(i)])
        residual = weight[rows(i)] * (summed - target[rows(i)])
        total[rows(i)] = residual
        for way in (1, -1):
            deliver(way, 0, i)
        out[me, rows(i)] = residual
    for d in (1, 2, 3, 4):
        for way, i in pairs:
            if d == 4 and not goes_far(way, i):
                continue
            wires.wait(("g", way, d - 1, i), out.at[turn(me, -d * way, NP), rows(i)], near[-way])
            if d < 3 or (d == 3 and goes_far(way, i)):
                deliver(way, d, i)
    wires.drain()


def exchange_pix(part, weight, target):
    count = 4 * (PIECES // 2 + 3 * PIECES)
    return pl.pallas_call(
        exchange_kernel,
        out_shape=jax.ShapeDtypeStruct(part.shape, f32),
        in_specs=[VMEM, VMEM, VMEM],
        out_specs=VMEM,
        scratch_shapes=[
            pltpu.VMEM((2, 4) + part.shape[1:], f32),
            pltpu.VMEM(part.shape[1:], f32),
            pltpu.SemaphoreType.DMA((count,)),
            pltpu.SemaphoreType.DMA((count,)),
        ],
        compiler_params=pltpu.CompilerParams(collective_id=2, has_side_effects=True),
        name="exchange_pix",
    )(part, weight, target)


def halves(value):
    high = value.astype(bf16)
    return high, (value - high.astype(f32)).astype(bf16)


def start_tiles(order, tiles, projector, held, sems):
    def one(k, _):
        pltpu.make_async_copy(projector.at[order[k]], held.at[k], sems.at[k // GROUP]).start()
        return 0

    lax.fori_loop(0, tiles, one, 0)


def wait_tiles(g, projector, held, sems):
    at = pl.ds(g * GROUP, GROUP)
    pltpu.make_async_copy(projector.at[pl.ds(0, GROUP)], held.at[at], sems.at[g]).wait()


def forward_kernel(
    first, ids, ray_counts, vol, projector, counts, part, weight, target, order, slots, cols, groups_out,
    held, sides, seen, slot_of, block_of, sems, seen_sem,
):
    n_tiles, blocks = ids.shape[0], counts.shape[0]
    width = counts.shape[1] // NP
    columns = vol.shape[0]
    fetch = pltpu.make_async_copy(counts.at[:, pl.ds(pl.multiple_of(first[0] * width, width), width)], seen, seen_sem)
    fetch.start()

    def find(b, k):
        live = lax.rem(b, MOST) < ray_counts[0, b // MOST]
        slot_of[b] = jnp.where(live, k, LIVE)
        block_of[jnp.where(live, k, LIVE)] = b
        return k + jnp.where(live, 1, 0)

    lax.fori_loop(0, blocks, find, 0, unroll=4)

    def scan(t, k):
        v = ids[t]
        slot = slot_of[v // columns]
        live = slot < LIVE
        order[k] = t
        slots[k] = slot
        cols[k] = lax.rem(v, columns)

        @pl.when(live)
        def _():
            pltpu.make_async_copy(projector.at[t], held.at[k], sems.at[k // GROUP]).start()

        return k + jnp.where(live, 1, 0)

    tiles = lax.fori_loop(0, n_tiles, scan, 0, unroll=4)
    groups = (tiles + GROUP - 1) // GROUP
    groups_out[0] = groups

    def pad(k, _):
        order[k] = 0
        slots[k] = LIVE
        cols[k] = 0
        pltpu.make_async_copy(projector.at[0], held.at[k], sems.at[k // GROUP]).start()
        return 0

    lax.fori_loop(tiles, groups * GROUP, pad, 0)

    lanes = vol.shape[2]

    def split(c, _):
        high, low = halves(vol[c])
        sides[c, :, 0:lanes] = high
        sides[c, :, lanes : 2 * lanes] = low
        sides[c, :, 2 * lanes : 3 * lanes] = high
        return 0

    lax.fori_loop(0, columns, split, 0, unroll=2)

    def clear(s, _):
        part[:, s] = jnp.zeros((NP, width, lanes), f32)
        return 0

    lax.fori_loop(0, LIVE + 1, clear, 0)
    fetch.wait()

    def weigh(s, _):
        n = seen[block_of[s]].astype(f32)
        weight[s] = n / BLANK
        target[s] = jnp.log(BLANK / n)
        return 0

    lax.fori_loop(0, LIVE, weigh, 0)

    def group(g, _):
        wait_tiles(g, projector, held, sems)
        products = []
        for u in range(GROUP):
            k = g * GROUP + u
            high, low = halves(held[k])
            products.append(
                lax.dot_general(
                    sides[cols[k]], jnp.concatenate([high, high, low], axis=1), NT, preferred_element_type=f32
                )
            )
        for u in range(GROUP):
            part[:, slots[g * GROUP + u]] += products[u].reshape(NP, width, lanes)
        return 0

    lax.fori_loop(0, groups, group, 0)


def forward(ids, ray_counts, vol, projector, counts):
    n_tiles, rays, lanes = projector.shape
    blocks, slices, _ = counts.shape
    width = slices // NP
    n_groups = -(-n_tiles // GROUP)
    padded = n_groups * GROUP
    first = lax.axis_index("pix").astype(i32).reshape(1)
    shape = jax.ShapeDtypeStruct
    return pl.pallas_call(
        forward_kernel,
        out_shape=(
            shape((NP, LIVE + 1, width, rays), f32),
            shape((LIVE, width, rays), f32),
            shape((LIVE, width, rays), f32),
            shape((padded,), i32),
            shape((padded,), i32),
            shape((padded,), i32),
            shape((1,), i32),
        ),
        in_specs=[SMEM, SMEM, SMEM, VMEM, ANY, ANY],
        out_specs=(VMEM, VMEM, VMEM, SMEM, SMEM, SMEM, SMEM),
        scratch_shapes=[
            pltpu.VMEM((padded, rays, lanes), f32),
            pltpu.VMEM((vol.shape[0], slices, 3 * lanes), bf16),
            pltpu.VMEM((blocks, width, rays), i32),
            pltpu.SMEM((blocks,), i32),
            pltpu.SMEM((LIVE + 1,), i32),
            pltpu.SemaphoreType.DMA((n_groups,)),
            pltpu.SemaphoreType.DMA(()),
        ],
        compiler_params=pltpu.CompilerParams(vmem_limit_bytes=56 << 20),
        name="forward",
    )(first, ids, ray_counts, vol, projector, counts)


def backward_kernel(order, slots, cols, groups_in, residual, projector, grad, held, sides, sems):
    groups = groups_in[0]
    start_tiles(order, groups * GROUP, projector, held, sems)
    live, slices, lanes = sides.shape[0] - 1, sides.shape[1], grad.shape[2]

    def split(s, _):
        high, low = halves(residual[:, s].reshape(slices, lanes))
        sides[s, :, 0:lanes] = high
        sides[s, :, lanes : 2 * lanes] = low
        sides[s, :, 2 * lanes : 3 * lanes] = high
        return 0

    lax.fori_loop(0, live, split, 0, unroll=2)
    sides[live] = jnp.zeros(sides.shape[1:], bf16)

    def clear(c, _):
        grad[c] = jnp.zeros(grad.shape[1:], f32)
        return 0

    lax.fori_loop(0, grad.shape[0], clear, 0)

    def group(g, _):
        wait_tiles(g, projector, held, sems)
        products = []
        for u in range(GROUP):
            k = g * GROUP + u
            high, low = halves(held[k])
            products.append(
                lax.dot_general(
                    sides[slots[k]], jnp.concatenate([high, high, low], axis=0), NN, preferred_element_type=f32
                )
            )
        for u in range(GROUP):
            grad[cols[g * GROUP + u]] += products[u]
        return 0

    lax.fori_loop(0, groups, group, 0)


def backward(order, slots, cols, groups, residual, projector, columns):
    n_tiles, rays, lanes = projector.shape
    padded = order.shape[0]
    slices = residual.shape[0] * residual.shape[2]
    return pl.pallas_call(
        backward_kernel,
        out_shape=jax.ShapeDtypeStruct((columns, slices, lanes), f32),
        in_specs=[SMEM, SMEM, SMEM, SMEM, VMEM, ANY],
        out_specs=VMEM,
        scratch_shapes=[
            pltpu.VMEM((padded, rays, lanes), f32),
            pltpu.VMEM((LIVE + 1, slices, 3 * rays), bf16),
            pltpu.SemaphoreType.DMA((padded // GROUP,)),
        ],
        compiler_params=pltpu.CompilerParams(vmem_limit_bytes=56 << 20),
        name="backward",
    )(order, slots, cols, groups, residual, projector)


def shards(volume, projector, tile_ids, counts, ray_counts):
    full = gather_ang(volume)
    part, weight, target, order, slots, cols, groups = forward(tile_ids, ray_counts, full, projector, counts)
    residual = exchange_pix(part, weight, target)
    terms = backward(order, slots, cols, groups, residual, projector, full.shape[0])
    gradient = scatter_ang(terms)
    return volume - STEP * gradient


def solution(mesh):
    placed = (
        P(("pix", "ang"), None, None),
        P(("pix", "ang"), None, None),
        P(("pix", "ang")),
        P("ang", None, None),
        P("ang", None),
    )
    return jax.shard_map(
        shards, mesh=mesh, in_specs=placed, out_specs=P(("pix", "ang"), None, None), check_vma=False
    )
```

```python
import functools

import jax
import jax.numpy as jnp
from jax import lax
from jax.experimental import pallas as pl
from jax.experimental.pallas import tpu as pltpu
from jax.sharding import PartitionSpec as P

f32, bf16, i32 = jnp.float32, jnp.bfloat16, jnp.int32
BLANK = 4096.0
STEP = 0.5
NP, NY, NX, NC = 8, 4, 4, 2
COLS = NY * NX * NC
MOST, LIVE = 4, 20
WIDTH = 16
HALF = 64
PIECES = 4
BATCH = 16
BUFFERS = 3
UNROLL = 8
LANES = 256
NN = (((1,), (0,)), ((), ()))
VMEM = pl.BlockSpec(memory_space=pltpu.VMEM)
SMEM = pl.BlockSpec(memory_space=pltpu.SMEM)
ANY = pl.BlockSpec(memory_space=pl.ANY)
MESH = pl.DeviceIdType.MESH
OFFSETS = sorted(
    ((dy, dx) for dy in range(NY) for dx in range(NX) if (dy, dx) != (0, 0)),
    key=lambda o: -(min(o[0], NY - o[0]) + min(o[1], NX - o[1])),
)


class Wires:
    def __init__(self, send, recv):
        self.send_sem, self.recv_sem, self.tags, self.started = send, recv, {}, []

    def copy(self, tag, src, dst, device):
        at = self.tags.setdefault(tag, len(self.tags))
        return pltpu.make_async_remote_copy(
            src_ref=src, dst_ref=dst, send_sem=self.send_sem.at[at], recv_sem=self.recv_sem.at[at],
            device_id=device, device_id_type=MESH,
        )

    def send(self, tag, src, dst, device):
        copy = self.copy(tag, src, dst, device)
        copy.start()
        self.started.append(copy)

    def wait(self, tag, dst, device):
        self.copy(tag, dst, dst, device).wait_recv()

    def drain(self):
        for copy in self.started:
            copy.wait_send()


def meet(devices):
    barrier = pltpu.get_barrier_semaphore()
    for device in devices:
        pl.semaphore_signal(barrier, inc=1, device_id=device, device_id_type=MESH)
    pl.semaphore_wait(barrier, len(devices))


def turn(i, by, n):
    return lax.rem(i + by + n, n)


def rel(d):
    return (d - 2) % NP


def halves(value):
    high = value.astype(bf16)
    return high, (value - high.astype(f32)).astype(bf16)


def dot(a, b):
    return lax.dot_general(a, b, NN, preferred_element_type=f32)


def turned(row):
    return jnp.transpose(jnp.broadcast_to(row, (LANES, LANES)))


def down(value):
    return jnp.sum(value, axis=0, keepdims=True, dtype=i32)


def tabulate(ids, ray_counts, work, table):
    n = ids.shape[1]
    work[...] = jnp.zeros(work.shape, i32)
    work[0:1, 0:n] = ids[...]
    v = work[0:1]
    lane = lax.broadcasted_iota(i32, (1, LANES), 1)
    lanes = lax.broadcasted_iota(i32, (LANES, LANES), 1)

    def slots_of(block):
        owner, j = block >> 2, block & (MOST - 1)
        held = jnp.zeros_like(block)
        before = jnp.zeros_like(block)
        running = jnp.int32(0)
        for o in range(NP):
            here = ray_counts[0, o]
            held = jnp.where(owner == o, here, held)
            before = jnp.where(owner == o, running, before)
            running = running + here
        return j < held, before + j

    live, slot = slots_of(v >> 5)
    live = live & (lane < n)
    col = v & (COLS - 1)
    slot = jnp.where(live, slot, 31)
    payload = turned(lane * 1024 + slot * 32 + col)
    for at, key, name in ((0, slot * 32 + col, slot), (1, col * 32 + slot, jnp.where(live, col, 63))):
        key = jnp.where(live, key, 2048 + lane)
        rank = down(jnp.where(turned(key) < key, 1, 0))
        table[at : at + 1] = down(jnp.where(turned(rank) == lanes, payload, 0))
        names = turned(name)
        count = down(jnp.where(names == lanes, 1, 0))
        upto = down(jnp.where(names <= lanes, 1, 0))
        table[at + 2 : at + 3] = jnp.where(count > 0, upto, 0)
    live, slot = slots_of(jnp.minimum(lane, NP * MOST - 1))
    names = turned(jnp.where(live & (lane < NP * MOST), slot, 63))
    which = lax.broadcasted_iota(i32, (LANES, LANES), 0)
    table[4:5] = down(jnp.where(names == lanes, which, 0))


def within(value, bound):
    return jnp.minimum(jnp.maximum(value, 0), bound - 1)


def step_kernel(
    ids, ray_counts, vol, projector, counts, out,
    rotated, full, stage, tiles, flipped, sides, back, sums, part, inbox, weight, target, residual, total, seen,
    grad, mine, terms, work, table, lists, tile_sems, other_sems, send, recv,
):
    me, ang = lax.axis_index("pix"), lax.axis_index("ang")
    core, x, y = lax.rem(ang, NC), lax.rem(ang // NC, NX), ang // (NC * NX)
    wires = Wires(send, recv)
    n_tiles = projector.shape[0]
    batches = n_tiles // BATCH

    def peer(dy, dx, c=core):
        return {"pix": me, "ang": (turn(y, dy, NY) * NX + turn(x, dx, NX)) * NC + c}

    partner = peer(0, 0, 1 - core)
    near = {way: {"pix": turn(me, way, NP), "ang": ang} for way in (1, -1)}

    def slices_of(i):
        return pl.ds(pl.multiple_of(turn(me, 2 + i, NP) * WIDTH, WIDTH), WIDTH)

    def chunk(k):
        return pl.ds(k * HALF, HALF)

    def fetch(b):
        return pltpu.make_async_copy(
            projector.at[pl.ds(b * BATCH, BATCH)], stage.at[b % BUFFERS], tile_sems.at[b]
        )

    look = pltpu.make_async_copy(counts.at[:, slices_of(rel(0))], seen, other_sems.at[0])
    for b in range(BUFFERS):
        fetch(b).start()
    look.start()
    for i in range(NP):
        rotated[i * WIDTH : (i + 1) * WIDTH] = vol[0, slices_of(i)]
    meet([peer(dy, dx) for dy, dx in OFFSETS] + [partner, near[1], near[-1]])

    for k in range(2):
        for dy, dx in OFFSETS:
            wires.send(("v", k, dy, dx), rotated.at[chunk(k)], full.at[y, x, core, chunk(k)], peer(dy, dx))
        wires.send(("p", k, 0, 0), rotated.at[chunk(k)], full.at[y, x, core, chunk(k)], partner)

    tabulate(ids, ray_counts, work, table)
    give = pltpu.make_async_copy(table, lists, other_sems.at[1])
    give.start()

    def prepare(b):
        fetch(b).wait()

        def one(t, _):
            value = stage[b % BUFFERS, t]
            high, low = halves(value)
            tiles[b * BATCH + t, 0] = high
            tiles[b * BATCH + t, 1] = low
            high, low = halves(jnp.transpose(value))
            flipped[b * BATCH + t, 0] = high
            flipped[b * BATCH + t, 1] = low
            return 0

        lax.fori_loop(0, BATCH, one, 0, unroll=2)
        if b + BUFFERS < batches:
            fetch(b + BUFFERS).start()

    def split_volume(k, yy, xx, c):
        high, low = halves(full[yy, xx, c, chunk(k)])
        at = (yy * NX + xx) * NC + c
        sides[k, at, 0:HALF] = high
        sides[k, at, HALF : 2 * HALF] = low

    def receive_volume(k):
        for dy, dx in OFFSETS:
            ref = full.at[turn(y, -dy, NY), turn(x, -dx, NX), core, chunk(k)]
            wires.wait(("v", k, dy, dx), ref, peer(-dy, -dx))
            wires.send(("p", k, dy, dx), ref, ref, partner)
            split_volume(k, turn(y, -dy, NY), turn(x, -dx, NX), core)

    def receive_partner(k):
        for dy, dx in [(0, 0)] + OFFSETS:
            ref = full.at[turn(y, -dy, NY), turn(x, -dx, NX), 1 - core, chunk(k)]
            wires.wait(("p", k, dy, dx), ref, partner)
            split_volume(k, turn(y, -dy, NY), turn(x, -dx, NX), 1 - core)

    def products(row, shift, left, k, right, first, count):
        def some(g, _):
            at = first + g * UNROLL
            running = sums[at]
            before = lists[row, jnp.maximum(at - 1, 0)]
            for u in range(UNROLL):
                entry = lists[row, at + u]
                name = (entry >> shift) & 31
                same = jnp.where(name == ((before >> shift) & 31), 1.0, 0.0)
                operand = (entry >> (5 - shift)) & 31
                t = within(entry >> 10, n_tiles)
                both = dot(left[k, operand], right[t, 0])
                value = both[0:HALF] + both[HALF : 2 * HALF] + dot(left[k, operand, 0:HALF], right[t, 1])
                running = value + running * same
                sums[at + u + 1] = running
                before = entry
            return 0

        lax.fori_loop(0, count // UNROLL, some, 0)

    def forward(k, first, count):
        products(0, 5, sides, k, flipped, first, count)

    def backward(k, first, count):
        products(1, 0, back, k, tiles, first, count)

    def take_part(k):
        def one(j, _):
            value = sums[within(lists[2, j], n_tiles + 1)]
            for i in range(4):
                part[4 * k + i, j] = value[i * WIDTH : (i + 1) * WIDTH]
            return 0

        lax.fori_loop(0, LIVE, one, 0, unroll=2)

    def weigh():
        look.wait()

        def one(j, _):
            n = seen[within(lists[4, j], NP * MOST)].astype(f32)
            weight[j] = n / BLANK
            target[j] = jnp.log(BLANK / n)
            return 0

        lax.fori_loop(0, LIVE, one, 0)

    size = LIVE // PIECES
    order = {1: list(range(PIECES)), -1: list(range(PIECES // 2, PIECES)) + list(range(PIECES // 2))}
    pairs = [(way, order[way][n]) for n in range(PIECES) for way in (1, -1)]

    def rows(i):
        return pl.ds(i * size, size)

    def goes_far(way, i):
        return (i < PIECES // 2) == (way == 1)

    def box(way, d, i):
        return inbox.at[0 if way == 1 else 1, d - 1, rows(i)]

    def pass_on(way, d, i, src):
        wires.send(("r", way, d, i), src, box(way, d, i), near[way])

    def start_sums():
        for way, i in pairs:
            if goes_far(way, i):
                pass_on(way, 4, i, part.at[rel(4), rows(i)])
        for way, i in pairs:
            if not goes_far(way, i):
                pass_on(way, 3, i, part.at[rel(3 * way), rows(i)])

    def relay_sums(d):
        for way, i in pairs:
            if d == 3 and not goes_far(way, i):
                continue
            wires.wait(("r", way, d + 1, i), box(way, d + 1, i), near[-way])
            w = 0 if way == 1 else 1
            inbox[w, d, rows(i)] += part[rel(d * way), rows(i)]
            pass_on(way, d, i, inbox.at[w, d, rows(i)])

    def deliver(way, d, i):
        ref = residual.at[rel(-d * way), rows(i)]
        there = residual.at[rel(-(d + 1) * way), rows(i)]
        src = ref if d else total.at[rows(i)]
        wires.send(("g", way, d, i), src, there, near[way])

    def finish_sums():
        for i in [pairs[2 * n][1] for n in range(PIECES)]:
            for way in (1, -1):
                wires.wait(("r", way, 1, i), box(way, 1, i), near[-way])
            summed = part[rel(0), rows(i)] + (inbox[0, 0, rows(i)] + inbox[1, 0, rows(i)])
            value = weight[rows(i)] * (summed - target[rows(i)])
            total[rows(i)] = value
            for way in (1, -1):
                deliver(way, 0, i)
            residual[rel(0), rows(i)] = value

    def relay_residual(d):
        for way, i in pairs:
            if d == 4 and not goes_far(way, i):
                continue
            wires.wait(("g", way, d - 1, i), residual.at[rel(-d * way), rows(i)], near[-way])
            if d < 3 or (d == 3 and goes_far(way, i)):
                deliver(way, d, i)

    def split_residual(k):
        def one(j, _):
            for i in range(4):
                high, low = halves(residual[4 * k + i, j])
                back[k, j, i * WIDTH : (i + 1) * WIDTH] = high
                back[k, j, HALF + i * WIDTH : HALF + (i + 1) * WIDTH] = low
            return 0

        lax.fori_loop(0, LIVE, one, 0, unroll=2)

    def start_grad(k):
        for c in range(COLS):
            grad[k, c // (NX * NC), (c // NC) % NX, c % NC] = sums[within(lists[3, c], n_tiles + 1)]
        wires.send(("q", k), grad.at[k, :, :, 1 - core], mine.at[k], partner)

    def spread_grad(k):
        wires.wait(("q", k), mine.at[k], partner)
        for n, (dy, dx) in enumerate(OFFSETS):
            yy, xx = turn(y, dy, NY), turn(x, dx, NX)
            mine[k, yy, xx] += grad[k, yy, xx, core]
            wires.send(("t", k, dy, dx), mine.at[k, yy, xx], terms.at[k, n], peer(dy, dx))

    def finish_grad(k):
        value = mine[k, y, x] + grad[k, y, x, core]
        for n, (dy, dx) in enumerate(OFFSETS):
            wires.wait(("t", k, dy, dx), terms.at[k, n], peer(-dy, -dx))
            value = value + terms[k, n]
        for i in range(4):
            out[0, slices_of(4 * k + i)] = value[i * WIDTH : (i + 1) * WIDTH]

    full[y, x, core] = rotated[...]
    for k in range(2):
        split_volume(k, y, x, core)
    sums[0] = jnp.zeros(sums.shape[1:], f32)
    for j in range(LIVE, 32):
        back[0, j] = jnp.zeros(back.shape[2:], bf16)
        back[1, j] = jnp.zeros(back.shape[2:], bf16)
    for b in range(batches - 3):
        prepare(b)
    receive_volume(0)
    for b in range(batches - 3, batches):
        prepare(b)
    give.wait()
    receive_partner(0)
    quarter = n_tiles // 4
    forward(0, 0, n_tiles)
    take_part(0)
    start_sums()
    receive_volume(1)
    receive_partner(1)
    forward(1, 0, 2 * quarter)
    weigh()
    relay_sums(3)
    forward(1, 2 * quarter, 2 * quarter)
    take_part(1)
    relay_sums(2)
    relay_sums(1)
    finish_sums()
    relay_residual(1)
    relay_residual(2)
    split_residual(1)
    backward(1, 0, 2 * quarter)
    relay_residual(3)
    backward(1, 2 * quarter, 2 * quarter)
    start_grad(1)
    relay_residual(4)
    split_residual(0)
    backward(0, 0, quarter)
    spread_grad(1)
    backward(0, quarter, 3 * quarter)
    start_grad(0)
    finish_grad(1)
    spread_grad(0)
    finish_grad(0)
    wires.drain()


def shards(volume, projector, tile_ids, counts, ray_counts):
    n_tiles, rays, lanes = projector.shape
    slices = volume.shape[1]
    n_sems = 2 * (2 * len(OFFSETS) + 1) + 4 * (PIECES // 2 + 3 * PIECES) + 2 * (len(OFFSETS) + 1)
    gradient = pl.pallas_call(
        step_kernel,
        out_shape=jax.ShapeDtypeStruct(volume.shape, f32),
        in_specs=[VMEM, SMEM, VMEM, ANY, ANY],
        out_specs=VMEM,
        scratch_shapes=[
            pltpu.VMEM((slices, lanes), f32),
            pltpu.VMEM((NY, NX, NC, slices, lanes), f32),
            pltpu.VMEM((BUFFERS, BATCH, rays, lanes), f32),
            pltpu.VMEM((n_tiles, 2, rays, lanes), bf16),
            pltpu.VMEM((n_tiles, 2, lanes, rays), bf16),
            pltpu.VMEM((2, COLS, 2 * HALF, lanes), bf16),
            pltpu.VMEM((2, 32, 2 * HALF, rays), bf16),
            pltpu.VMEM((n_tiles + 1, HALF, lanes), f32),
            pltpu.VMEM((NP, LIVE, WIDTH, rays), f32),
            pltpu.VMEM((2, 4, LIVE, WIDTH, rays), f32),
            pltpu.VMEM((LIVE, WIDTH, rays), f32),
            pltpu.VMEM((LIVE, WIDTH, rays), f32),
            pltpu.VMEM((NP, LIVE, WIDTH, rays), f32),
            pltpu.VMEM((LIVE, WIDTH, rays), f32),
            pltpu.VMEM((counts.shape[0], WIDTH, rays), i32),
            pltpu.VMEM((2, NY, NX, NC, HALF, lanes), f32),
            pltpu.VMEM((2, NY, NX, HALF, lanes), f32),
            pltpu.VMEM((2, len(OFFSETS), HALF, lanes), f32),
            pltpu.VMEM((8, LANES), i32),
            pltpu.VMEM((8, LANES), i32),
            pltpu.SMEM((8, LANES), i32),
            pltpu.SemaphoreType.DMA((n_tiles // BATCH,)),
            pltpu.SemaphoreType.DMA((2,)),
            pltpu.SemaphoreType.DMA((n_sems,)),
            pltpu.SemaphoreType.DMA((n_sems,)),
        ],
        compiler_params=pltpu.CompilerParams(
            collective_id=0, has_side_effects=True, vmem_limit_bytes=62 << 20
        ),
        name="step",
    )(tile_ids.reshape(1, n_tiles), ray_counts, volume, projector, counts)
    return volume - STEP * gradient


def solution(mesh):
    placed = (
        P(("pix", "ang"), None, None),
        P(("pix", "ang"), None, None),
        P(("pix", "ang")),
        P("ang", None, None),
        P("ang", None),
    )
    return jax.shard_map(
        shards, mesh=mesh, in_specs=placed, out_specs=P(("pix", "ang"), None, None), check_vma=False
    )
```

```python
import functools

import jax
import jax.numpy as jnp
from jax import lax
from jax.experimental import pallas as pl
from jax.experimental.pallas import tpu as pltpu
from jax.sharding import PartitionSpec as P

f32, bf16, i32 = jnp.float32, jnp.bfloat16, jnp.int32
BLANK = 4096.0
STEP = 0.5
NP, NY, NX, NC = 8, 4, 4, 2
COLS = NY * NX * NC
MOST, LIVE = 4, 20
WIDTH = 16
PLACES = (3, 4, -3, 2, -2, -1, 0, 1)
CHUNKS = ((0, 3), (3, 2), (5, 3))
PIECES = 4
BATCH = 16
BUFFERS = 3
UNROLL = 40
LANES = 256
NN = (((1,), (0,)), ((), ()))
VMEM = pl.BlockSpec(memory_space=pltpu.VMEM)
SMEM = pl.BlockSpec(memory_space=pltpu.SMEM)
ANY = pl.BlockSpec(memory_space=pl.ANY)
MESH = pl.DeviceIdType.MESH
OFFSETS = sorted(
    ((dy, dx) for dy in range(NY) for dx in range(NX) if (dy, dx) != (0, 0)),
    key=lambda o: -(min(o[0], NY - o[0]) + min(o[1], NX - o[1])),
)
BY_ROW = [(dy, dx) for dy in (2, 1, 3, 0) for dx in (2, 1, 3, 0) if (dy, dx) != (0, 0)]


class Wires:
    def __init__(self, send, recv):
        self.send_sem, self.recv_sem, self.tags, self.started = send, recv, {}, []

    def copy(self, tag, src, dst, device):
        at = self.tags.setdefault(tag, len(self.tags))
        return pltpu.make_async_remote_copy(
            src_ref=src, dst_ref=dst, send_sem=self.send_sem.at[at], recv_sem=self.recv_sem.at[at],
            device_id=device, device_id_type=MESH,
        )

    def send(self, tag, src, dst, device):
        copy = self.copy(tag, src, dst, device)
        copy.start()
        self.started.append(copy)

    def wait(self, tag, dst, device):
        self.copy(tag, dst, dst, device).wait_recv()

    def drain(self):
        for copy in self.started:
            copy.wait_send()


def greet(devices):
    barrier = pltpu.get_barrier_semaphore()
    for device in devices:
        pl.semaphore_signal(barrier, inc=1, device_id=device, device_id_type=MESH)


def turn(i, by, n):
    return lax.rem(i + by + n, n)


def rel(d):
    return [p % NP for p in PLACES].index(d % NP)


def halves(value):
    high = value.astype(bf16)
    return high, (value - high.astype(f32)).astype(bf16)


def dot(a, b):
    return lax.dot_general(a, b, NN, preferred_element_type=f32)


def turned(row):
    return jnp.transpose(jnp.broadcast_to(row, (LANES, LANES)))


def down(value):
    return jnp.sum(value, axis=0, keepdims=True, dtype=i32)


def tabulate(ids, ray_counts, work, table):
    n = ids.shape[1]
    work[...] = jnp.zeros(work.shape, i32)
    work[0:1, 0:n] = ids[...]
    v = work[0:1]
    lane = lax.broadcasted_iota(i32, (1, LANES), 1)
    lanes = lax.broadcasted_iota(i32, (LANES, LANES), 1)

    def slots_of(block):
        owner, j = block >> 2, block & (MOST - 1)
        held = jnp.zeros_like(block)
        before = jnp.zeros_like(block)
        running = jnp.int32(0)
        for o in range(NP):
            here = ray_counts[0, o]
            held = jnp.where(owner == o, here, held)
            before = jnp.where(owner == o, running, before)
            running = running + here
        return j < held, before + j

    live, slot = slots_of(v >> 5)
    live = live & (lane < n)
    col = v & (COLS - 1)
    slot = jnp.where(live, slot, 31)
    payload = turned(lane * 1024 + slot * 32 + col)
    for at, key, name in ((0, slot * 32 + col, slot), (1, col * 32 + slot, jnp.where(live, col, 63))):
        key = jnp.where(live, key, 2048 + lane)
        rank = down(jnp.where(turned(key) < key, 1, 0))
        table[at : at + 1] = down(jnp.where(turned(rank) == lanes, payload, 0))
        names = turned(name)
        count = down(jnp.where(names == lanes, 1, 0))
        upto = down(jnp.where(names <= lanes, 1, 0))
        table[at + 2 : at + 3] = jnp.where(count > 0, upto, 0)
    live, slot = slots_of(jnp.minimum(lane, NP * MOST - 1))
    names = turned(jnp.where(live & (lane < NP * MOST), slot, 63))
    which = lax.broadcasted_iota(i32, (LANES, LANES), 0)
    table[4:5] = down(jnp.where(names == lanes, which, 0))


def within(value, bound):
    return jnp.minimum(jnp.maximum(value, 0), bound - 1)


def step_kernel(
    ids, ray_counts, vol, projector, counts, out,
    rotated, full, stage, tiles, flipped, side0, side1, side2, back0, back1, back2, sums, part, inbox, weight, target,
    residual, total, seen, grad, mine, terms, work, table, lists, tile_sems, other_sems, send, recv,
):
    me, ang = lax.axis_index("pix"), lax.axis_index("ang")
    core, x, y = lax.rem(ang, NC), lax.rem(ang // NC, NX), ang // (NC * NX)
    wires = Wires(send, recv)
    sides, back = (side0, side1, side2), (back0, back1, back2)
    n_tiles = projector.shape[0]
    batches = n_tiles // BATCH

    def peer(dy, dx, c=core):
        return {"pix": me, "ang": (turn(y, dy, NY) * NX + turn(x, dx, NX)) * NC + c}

    partner = peer(0, 0, 1 - core)
    near = {way: {"pix": turn(me, way, NP), "ang": ang} for way in (1, -1)}
    friends = [peer(dy, dx) for dy, dx in OFFSETS] + [partner, near[1], near[-1]]
    greet(friends)

    def slices_of(i):
        return pl.ds(pl.multiple_of(turn(me, PLACES[i], NP) * WIDTH, WIDTH), WIDTH)

    def length(k):
        return CHUNKS[k][1] * WIDTH

    def chunk(k):
        return pl.ds(CHUNKS[k][0] * WIDTH, length(k))

    def fetch(b):
        return pltpu.make_async_copy(
            projector.at[pl.ds(b * BATCH, BATCH)], stage.at[b % BUFFERS], tile_sems.at[b]
        )

    look = pltpu.make_async_copy(counts.at[:, slices_of(rel(0))], seen, other_sems.at[0])
    for b in range(BUFFERS):
        fetch(b).start()
    look.start()
    for i in range(NP):
        rotated[i * WIDTH : (i + 1) * WIDTH] = vol[0, slices_of(i)]
    pl.semaphore_wait(pltpu.get_barrier_semaphore(), len(friends))

    for k in range(len(CHUNKS)):
        for dy, dx in OFFSETS:
            wires.send(("v", k, dy, dx), rotated.at[chunk(k)], full.at[y, x, core, chunk(k)], peer(dy, dx))
        wires.send(("p", k, 0, 0), rotated.at[chunk(k)], full.at[y, x, core, chunk(k)], partner)

    tabulate(ids, ray_counts, work, table)
    give = pltpu.make_async_copy(table, lists, other_sems.at[1])
    give.start()

    def prepare(b):
        fetch(b).wait()

        def one(t, _):
            high, low = halves(stage[b % BUFFERS, t])
            tiles[b * BATCH + t, 0] = high
            tiles[b * BATCH + t, 1] = low
            flipped[b * BATCH + t, 0] = jnp.transpose(high)
            flipped[b * BATCH + t, 1] = jnp.transpose(low)
            return 0

        lax.fori_loop(0, BATCH, one, 0, unroll=8)
        if b + BUFFERS < batches:
            fetch(b + BUFFERS).start()

    def split_volume(k, value, yy, xx, c):
        high, low = halves(value)
        at = (yy * NX + xx) * NC + c
        sides[k][at, 0 : length(k)] = high
        sides[k][at, length(k) : 2 * length(k)] = low

    def receive_volume(k):
        for dy, dx in OFFSETS:
            yy, xx = turn(y, -dy, NY), turn(x, -dx, NX)
            ref = full.at[yy, xx, core, chunk(k)]
            wires.wait(("v", k, dy, dx), ref, peer(-dy, -dx))
            wires.send(("p", k, dy, dx), ref, ref, partner)
            split_volume(k, ref[...], yy, xx, core)

    def receive_partner(k):
        for dy, dx in [(0, 0)] + OFFSETS:
            yy, xx = turn(y, -dy, NY), turn(x, -dx, NX)
            ref = full.at[yy, xx, 1 - core, chunk(k)]
            wires.wait(("p", k, dy, dx), ref, partner)
            split_volume(k, ref[...], yy, xx, 1 - core)

    def products(row, shift, left, m, right, first, count):
        def some(g, _):
            at = first + g * UNROLL
            running = sums[at, 0:m]
            before = lists[row, jnp.maximum(at - 1, 0)]
            for u in range(UNROLL):
                entry = lists[row, at + u]
                name = (entry >> shift) & 31
                same = jnp.where(name == ((before >> shift) & 31), 1.0, 0.0)
                operand = (entry >> (5 - shift)) & 31
                t = within(entry >> 10, n_tiles)
                both = dot(left[operand], right[t, 0])
                value = both[0:m] + both[m : 2 * m] + dot(left[operand, 0:m], right[t, 1])
                running = value + running * same
                sums[at + u + 1, 0:m] = running
                before = entry
            return 0

        lax.fori_loop(0, count // UNROLL, some, 0)

    def forward(k, first, count):
        products(0, 5, sides[k], length(k), flipped, first, count)

    def backward(k, first, count):
        products(1, 0, back[k], length(k), tiles, first, count)

    def take_part(k):
        place, number = CHUNKS[k]

        def one(j, _):
            at = within(lists[2, j], n_tiles + 1)
            for i in range(number):
                part[place + i, j] = sums[at, i * WIDTH : (i + 1) * WIDTH]
            return 0

        lax.fori_loop(0, LIVE, one, 0, unroll=4)

    def weigh():
        look.wait()

        def one(j, _):
            n = seen[within(lists[4, j], NP * MOST)].astype(f32)
            weight[j] = n / BLANK
            target[j] = jnp.log(BLANK / n)
            return 0

        lax.fori_loop(0, LIVE, one, 0, unroll=2)

    size = LIVE // PIECES
    order = {1: list(range(PIECES)), -1: list(range(PIECES // 2, PIECES)) + list(range(PIECES // 2))}
    pairs = [(way, order[way][n]) for n in range(PIECES) for way in (1, -1)]

    def rows(i):
        return pl.ds(i * size, size)

    def goes_far(way, i):
        return (i < PIECES // 2) == (way == 1)

    def box(way, d, i):
        return inbox.at[0 if way == 1 else 1, d - 1, rows(i)]

    def pass_on(way, d, i, src):
        wires.send(("r", way, d, i), src, box(way, d, i), near[way])

    def start_sums():
        for way, i in pairs:
            if goes_far(way, i):
                pass_on(way, 4, i, part.at[rel(4), rows(i)])
        for way, i in pairs:
            if not goes_far(way, i):
                pass_on(way, 3, i, part.at[rel(3 * way), rows(i)])

    def relay_sums(d, far):
        for way, i in pairs:
            if goes_far(way, i) != far:
                continue
            wires.wait(("r", way, d + 1, i), box(way, d + 1, i), near[-way])
            w = 0 if way == 1 else 1
            inbox[w, d, rows(i)] += part[rel(d * way), rows(i)]
            pass_on(way, d, i, inbox.at[w, d, rows(i)])

    def deliver(way, d, i):
        ref = residual.at[rel(-d * way), rows(i)]
        there = residual.at[rel(-(d + 1) * way), rows(i)]
        src = ref if d else total.at[rows(i)]
        wires.send(("g", way, d, i), src, there, near[way])

    def finish_sums():
        for i in [pairs[2 * n][1] for n in range(PIECES)]:
            for way in (1, -1):
                wires.wait(("r", way, 1, i), box(way, 1, i), near[-way])
            summed = part[rel(0), rows(i)] + (inbox[0, 0, rows(i)] + inbox[1, 0, rows(i)])
            value = weight[rows(i)] * (summed - target[rows(i)])
            total[rows(i)] = value
            for way in (1, -1):
                deliver(way, 0, i)
            residual[rel(0), rows(i)] = value

    def relay_residual(d, some=pairs, near_too=True):
        for way, i in some:
            if (d == 4 or not near_too) and not goes_far(way, i):
                continue
            wires.wait(("g", way, d - 1, i), residual.at[rel(-d * way), rows(i)], near[-way])
            if d < 3 or (d == 3 and goes_far(way, i)):
                deliver(way, d, i)

    def split_residual(k):
        place, number = CHUNKS[k]

        def one(j, _):
            for i in range(number):
                high, low = halves(residual[place + i, j])
                back[k][j, i * WIDTH : (i + 1) * WIDTH] = high
                back[k][j, length(k) + i * WIDTH : length(k) + (i + 1) * WIDTH] = low
            return 0

        lax.fori_loop(0, LIVE, one, 0, unroll=4)

    def start_grad(k):
        for dy in (2, 1, 3, 0):
            yy = turn(y, dy, NY)
            for n in range(NX * NC):
                at = within(lists[3, yy * (NX * NC) + n], n_tiles + 1)
                grad[yy, n // NC, n % NC, chunk(k)] = sums[at, 0 : length(k)]
            wires.send(("q", k, dy), grad.at[yy, :, 1 - core, chunk(k)], mine.at[yy, :, chunk(k)], partner)

    def spread_grad(k):
        for dy in (2, 1, 3, 0):
            yy = turn(y, dy, NY)
            wires.wait(("q", k, dy), mine.at[yy, :, chunk(k)], partner)
            for n, (to_y, dx) in enumerate(BY_ROW):
                if to_y == dy:
                    xx = turn(x, dx, NX)
                    mine[yy, xx, chunk(k)] += grad[yy, xx, core, chunk(k)]
                    wires.send(("t", k, n), mine.at[yy, xx, chunk(k)], terms.at[n, chunk(k)], peer(dy, dx))

    def finish_grad(k):
        value = mine[y, x, chunk(k)] + grad[y, x, core, chunk(k)]
        for n, (dy, dx) in enumerate(BY_ROW):
            wires.wait(("t", k, n), terms.at[n, chunk(k)], peer(-dy, -dx))
            value = value + terms[n, chunk(k)]
        place, number = CHUNKS[k]
        for i in range(number):
            out[0, slices_of(place + i)] = value[i * WIDTH : (i + 1) * WIDTH]

    quarter = n_tiles // 4
    for k in range(len(CHUNKS)):
        split_volume(k, rotated[chunk(k)], y, x, core)
        for j in range(LIVE, 32):
            back[k][j] = jnp.zeros(back[k].shape[1:], bf16)
    sums[0] = jnp.zeros(sums.shape[1:], f32)
    for b in range(batches):
        prepare(b)
    receive_volume(0)
    give.wait()
    receive_partner(0)
    forward(0, 0, n_tiles)
    take_part(0)
    start_sums()
    receive_volume(1)
    weigh()
    receive_partner(1)
    forward(1, 0, 2 * quarter)
    relay_sums(3, True)
    receive_volume(2)
    forward(1, 2 * quarter, 2 * quarter)
    take_part(1)
    relay_sums(2, False)
    receive_partner(2)
    forward(2, 0, quarter)
    relay_sums(2, True)
    forward(2, quarter, 3 * quarter)
    take_part(2)
    relay_sums(1, False)
    relay_sums(1, True)
    finish_sums()
    relay_residual(1)
    split_residual(2)
    backward(2, 0, quarter)
    relay_residual(2, pairs[0:2])
    relay_residual(2, pairs[2:4])
    backward(2, quarter, quarter)
    relay_residual(2, pairs[4:6])
    backward(2, 2 * quarter, 2 * quarter)
    relay_residual(2, pairs[6:8])
    start_grad(2)
    split_residual(1)
    relay_residual(3, pairs[0:4], near_too=False)
    backward(1, 0, 2 * quarter)
    spread_grad(2)
    backward(1, 2 * quarter, 2 * quarter)
    start_grad(1)
    relay_residual(3, pairs[4:8])
    relay_residual(4)
    split_residual(0)
    backward(0, 0, quarter)
    spread_grad(1)
    backward(0, quarter, 3 * quarter)
    start_grad(0)
    finish_grad(2)
    finish_grad(1)
    spread_grad(0)
    finish_grad(0)
    wires.drain()


def shards(volume, projector, tile_ids, counts, ray_counts):
    n_tiles, rays, lanes = projector.shape
    slices = volume.shape[1]
    n_sems = len(CHUNKS) * (3 * len(OFFSETS) + 1 + NY) + 4 * (PIECES // 2 + 3 * PIECES)
    lengths = [number * WIDTH for _, number in CHUNKS]
    gradient = pl.pallas_call(
        step_kernel,
        out_shape=jax.ShapeDtypeStruct(volume.shape, f32),
        in_specs=[VMEM, SMEM, VMEM, ANY, ANY],
        out_specs=VMEM,
        scratch_shapes=[
            pltpu.VMEM((slices, lanes), f32),
            pltpu.VMEM((NY, NX, NC, slices, lanes), f32),
            pltpu.VMEM((BUFFERS, BATCH, rays, lanes), f32),
            pltpu.VMEM((n_tiles, 2, rays, lanes), bf16),
            pltpu.VMEM((n_tiles, 2, lanes, rays), bf16),
            *[pltpu.VMEM((COLS, 2 * m, lanes), bf16) for m in lengths],
            *[pltpu.VMEM((32, 2 * m, rays), bf16) for m in lengths],
            pltpu.VMEM((n_tiles + 1, max(lengths), lanes), f32),
            pltpu.VMEM((NP, LIVE, WIDTH, rays), f32),
            pltpu.VMEM((2, 4, LIVE, WIDTH, rays), f32),
            pltpu.VMEM((LIVE, WIDTH, rays), f32),
            pltpu.VMEM((LIVE, WIDTH, rays), f32),
            pltpu.VMEM((NP, LIVE, WIDTH, rays), f32),
            pltpu.VMEM((LIVE, WIDTH, rays), f32),
            pltpu.VMEM((counts.shape[0], WIDTH, rays), i32),
            pltpu.VMEM((NY, NX, NC, slices, lanes), f32),
            pltpu.VMEM((NY, NX, slices, lanes), f32),
            pltpu.VMEM((len(OFFSETS), slices, lanes), f32),
            pltpu.VMEM((8, LANES), i32),
            pltpu.VMEM((8, LANES), i32),
            pltpu.SMEM((8, LANES), i32),
            pltpu.SemaphoreType.DMA((n_tiles // BATCH,)),
            pltpu.SemaphoreType.DMA((2,)),
            pltpu.SemaphoreType.DMA((n_sems,)),
            pltpu.SemaphoreType.DMA((n_sems,)),
        ],
        compiler_params=pltpu.CompilerParams(
            collective_id=0, has_side_effects=True, vmem_limit_bytes=62 << 20
        ),
        name="step",
    )(tile_ids.reshape(1, n_tiles), ray_counts, volume, projector, counts)
    return volume - STEP * gradient


def solution(mesh):
    placed = (
        P(("pix", "ang"), None, None),
        P(("pix", "ang"), None, None),
        P(("pix", "ang")),
        P("ang", None, None),
        P("ang", None),
    )
    return jax.shard_map(
        shards, mesh=mesh, in_specs=placed, out_specs=P(("pix", "ang"), None, None), check_vma=False
    )
```

```python
import functools

import jax
import jax.numpy as jnp
from jax import lax
from jax.experimental import pallas as pl
from jax.experimental.pallas import tpu as pltpu
from jax.sharding import PartitionSpec as P

f32, bf16, i32 = jnp.float32, jnp.bfloat16, jnp.int32
BLANK = 4096.0
STEP = 0.5
NP, NY, NX, NC = 8, 4, 4, 2
COLS = NY * NX * NC
MOST, LIVE = 4, 20
WIDTH = 16
PLACES = (3, 4, -3, 2, -2, -1, 0, 1)
CHUNKS = ((0, 3), (3, 2), (5, 3))
PIECES = 4
BATCH = 16
BUFFERS = 3
UNROLL = 40
LANES = 256
NN = (((1,), (0,)), ((), ()))
VMEM = pl.BlockSpec(memory_space=pltpu.VMEM)
SMEM = pl.BlockSpec(memory_space=pltpu.SMEM)
ANY = pl.BlockSpec(memory_space=pl.ANY)
MESH = pl.DeviceIdType.MESH
OFFSETS = sorted(
    ((dy, dx) for dy in range(NY) for dx in range(NX) if (dy, dx) != (0, 0)),
    key=lambda o: -(min(o[0], NY - o[0]) + min(o[1], NX - o[1])),
)
BY_ROW = [(dy, dx) for dy in (2, 1, 3, 0) for dx in (2, 1, 3, 0) if (dy, dx) != (0, 0)]


class Wires:
    def __init__(self, send, recv):
        self.send_sem, self.recv_sem, self.tags, self.started = send, recv, {}, []

    def copy(self, tag, src, dst, device):
        at = self.tags.setdefault(tag, len(self.tags))
        return pltpu.make_async_remote_copy(
            src_ref=src, dst_ref=dst, send_sem=self.send_sem.at[at], recv_sem=self.recv_sem.at[at],
            device_id=device, device_id_type=MESH,
        )

    def send(self, tag, src, dst, device):
        copy = self.copy(tag, src, dst, device)
        copy.start()
        self.started.append(copy)

    def wait(self, tag, dst, device):
        self.copy(tag, dst, dst, device).wait_recv()

    def drain(self):
        for copy in self.started:
            copy.wait_send()


def greet(devices):
    barrier = pltpu.get_barrier_semaphore()
    for device in devices:
        pl.semaphore_signal(barrier, inc=1, device_id=device, device_id_type=MESH)


def turn(i, by, n):
    return lax.rem(i + by + n, n)


def rel(d):
    return [p % NP for p in PLACES].index(d % NP)


def halves(value):
    high = value.astype(bf16)
    return high, (value - high.astype(f32)).astype(bf16)


def dot(a, b):
    return lax.dot_general(a, b, NN, preferred_element_type=f32)


def turned(row):
    return jnp.transpose(jnp.broadcast_to(row, (LANES, LANES)))


def down(value):
    return jnp.sum(value, axis=0, keepdims=True, dtype=i32)


def tabulate(ids, ray_counts, work, table):
    n = ids.shape[1]
    work[...] = jnp.zeros(work.shape, i32)
    work[0:1, 0:n] = ids[...]
    v = work[0:1]
    lane = lax.broadcasted_iota(i32, (1, LANES), 1)
    lanes = lax.broadcasted_iota(i32, (LANES, LANES), 1)

    def slots_of(block):
        owner, j = block >> 2, block & (MOST - 1)
        held = jnp.zeros_like(block)
        before = jnp.zeros_like(block)
        running = jnp.int32(0)
        for o in range(NP):
            here = ray_counts[0, o]
            held = jnp.where(owner == o, here, held)
            before = jnp.where(owner == o, running, before)
            running = running + here
        return j < held, before + j

    live, slot = slots_of(v >> 5)
    live = live & (lane < n)
    col = v & (COLS - 1)
    slot = jnp.where(live, slot, 31)
    payload = turned(lane * 1024 + slot * 32 + col)
    for at, key, name in ((0, slot * 32 + col, slot), (1, col * 32 + slot, jnp.where(live, col, 63))):
        key = jnp.where(live, key, 2048 + lane)
        rank = down(jnp.where(turned(key) < key, 1, 0))
        table[at : at + 1] = down(jnp.where(turned(rank) == lanes, payload, 0))
        names = turned(name)
        count = down(jnp.where(names == lanes, 1, 0))
        upto = down(jnp.where(names <= lanes, 1, 0))
        table[at + 2 : at + 3] = jnp.where(count > 0, upto, 0)
    live, slot = slots_of(jnp.minimum(lane, NP * MOST - 1))
    names = turned(jnp.where(live & (lane < NP * MOST), slot, 63))
    which = lax.broadcasted_iota(i32, (LANES, LANES), 0)
    table[4:5] = down(jnp.where(names == lanes, which, 0))


def within(value, bound):
    return jnp.minimum(jnp.maximum(value, 0), bound - 1)


def step_kernel(
    ids, ray_counts, vol, projector, counts, out,
    rotated, full, stage, tiles, flipped, side0, side1, side2, back0, back1, back2, sums, part, inbox, weight, target,
    residual, total, seen, grad, mine, terms, work, table, lists, tile_sems, other_sems, send, recv,
):
    me, ang = lax.axis_index("pix"), lax.axis_index("ang")
    core, x, y = lax.rem(ang, NC), lax.rem(ang // NC, NX), ang // (NC * NX)
    wires = Wires(send, recv)
    sides, back = (side0, side1, side2), (back0, back1, back2)
    n_tiles = projector.shape[0]
    batches = n_tiles // BATCH

    def peer(dy, dx, c=core):
        return {"pix": me, "ang": (turn(y, dy, NY) * NX + turn(x, dx, NX)) * NC + c}

    partner = peer(0, 0, 1 - core)
    near = {way: {"pix": turn(me, way, NP), "ang": ang} for way in (1, -1)}
    friends = [peer(dy, dx) for dy, dx in OFFSETS] + [partner, near[1], near[-1]]
    greet(friends)

    def slices_of(i):
        return pl.ds(pl.multiple_of(turn(me, PLACES[i], NP) * WIDTH, WIDTH), WIDTH)

    def length(k):
        return CHUNKS[k][1] * WIDTH

    def chunk(k):
        return pl.ds(CHUNKS[k][0] * WIDTH, length(k))

    def fetch(b):
        return pltpu.make_async_copy(
            projector.at[pl.ds(b * BATCH, BATCH)], stage.at[b % BUFFERS], tile_sems.at[b]
        )

    look = pltpu.make_async_copy(counts.at[:, slices_of(rel(0))], seen, other_sems.at[0])
    for b in range(BUFFERS):
        fetch(b).start()
    look.start()
    for i in range(NP):
        rotated[i * WIDTH : (i + 1) * WIDTH] = vol[0, slices_of(i)]
    pl.semaphore_wait(pltpu.get_barrier_semaphore(), len(friends))

    for k in range(len(CHUNKS)):
        for dy, dx in OFFSETS:
            wires.send(("v", k, dy, dx), rotated.at[chunk(k)], full.at[y, x, core, chunk(k)], peer(dy, dx))
        wires.send(("p", k, 0, 0), rotated.at[chunk(k)], full.at[y, x, core, chunk(k)], partner)

    tabulate(ids, ray_counts, work, table)
    give = pltpu.make_async_copy(table, lists, other_sems.at[1])
    give.start()

    def prepare(b):
        fetch(b).wait()

        def one(t, _):
            high, low = halves(stage[b % BUFFERS, t])
            tiles[b * BATCH + t, 0] = high
            tiles[b * BATCH + t, 1] = low
            flipped[b * BATCH + t, 0] = jnp.transpose(high)
            flipped[b * BATCH + t, 1] = jnp.transpose(low)
            return 0

        lax.fori_loop(0, BATCH, one, 0, unroll=8)
        if b + BUFFERS < batches:
            fetch(b + BUFFERS).start()

    def split_volume(k, value, yy, xx, c):
        high, low = halves(value)
        at = (yy * NX + xx) * NC + c
        sides[k][at, 0 : length(k)] = high
        sides[k][at, length(k) : 2 * length(k)] = low

    def receive_volume(k):
        for dy, dx in OFFSETS:
            yy, xx = turn(y, -dy, NY), turn(x, -dx, NX)
            ref = full.at[yy, xx, core, chunk(k)]
            wires.wait(("v", k, dy, dx), ref, peer(-dy, -dx))
            wires.send(("p", k, dy, dx), ref, ref, partner)
            split_volume(k, ref[...], yy, xx, core)

    def receive_partner(k):
        for dy, dx in [(0, 0)] + OFFSETS:
            yy, xx = turn(y, -dy, NY), turn(x, -dx, NX)
            ref = full.at[yy, xx, 1 - core, chunk(k)]
            wires.wait(("p", k, dy, dx), ref, partner)
            split_volume(k, ref[...], yy, xx, 1 - core)

    def products(row, shift, left, m, right, first, count):
        def some(g, _):
            at = first + g * UNROLL
            running = sums[at, 0:m]
            before = lists[row, jnp.maximum(at - 1, 0)]
            for u in range(UNROLL):
                entry = lists[row, at + u]
                name = (entry >> shift) & 31
                same = jnp.where(name == ((before >> shift) & 31), 1.0, 0.0)
                operand = (entry >> (5 - shift)) & 31
                t = within(entry >> 10, n_tiles)
                both = dot(left[operand], right[t, 0])
                value = both[0:m] + both[m : 2 * m] + dot(left[operand, 0:m], right[t, 1])
                running = value + running * same
                sums[at + u + 1, 0:m] = running
                before = entry
            return 0

        lax.fori_loop(0, count // UNROLL, some, 0)

    def forward(k, first, count):
        products(0, 5, sides[k], length(k), flipped, first, count)

    def backward(k, first, count):
        products(1, 0, back[k], length(k), tiles, first, count)

    def take_part(k):
        place, number = CHUNKS[k]

        def one(j, _):
            at = within(lists[2, j], n_tiles + 1)
            for i in range(number):
                part[place + i, j] = sums[at, i * WIDTH : (i + 1) * WIDTH]
            return 0

        lax.fori_loop(0, LIVE, one, 0, unroll=4)

    def weigh():
        look.wait()

        def one(j, _):
            n = seen[within(lists[4, j], NP * MOST)].astype(f32)
            weight[j] = n / BLANK
            target[j] = jnp.log(BLANK / n)
            return 0

        lax.fori_loop(0, LIVE, one, 0, unroll=2)

    size = LIVE // PIECES
    order = {1: list(range(PIECES)), -1: list(range(PIECES // 2, PIECES)) + list(range(PIECES // 2))}
    pairs = [(way, order[way][n]) for n in range(PIECES) for way in (1, -1)]

    def rows(i):
        return pl.ds(i * size, size)

    def goes_far(way, i):
        return (i < PIECES // 2) == (way == 1)

    def box(way, d, i):
        return inbox.at[0 if way == 1 else 1, d - 1, rows(i)]

    def pass_on(way, d, i, src):
        wires.send(("r", way, d, i), src, box(way, d, i), near[way])

    def start_sums():
        for way, i in pairs:
            if goes_far(way, i):
                pass_on(way, 4, i, part.at[rel(4), rows(i)])
        for way, i in pairs:
            if not goes_far(way, i):
                pass_on(way, 3, i, part.at[rel(3 * way), rows(i)])

    def relay_sums(d, far):
        for way, i in pairs:
            if goes_far(way, i) != far:
                continue
            wires.wait(("r", way, d + 1, i), box(way, d + 1, i), near[-way])
            w = 0 if way == 1 else 1
            inbox[w, d, rows(i)] += part[rel(d * way), rows(i)]
            pass_on(way, d, i, inbox.at[w, d, rows(i)])

    def deliver(way, d, i):
        ref = residual.at[rel(-d * way), rows(i)]
        there = residual.at[rel(-(d + 1) * way), rows(i)]
        src = ref if d else total.at[rows(i)]
        wires.send(("g", way, d, i), src, there, near[way])

    def finish_sums():
        for i in [pairs[2 * n][1] for n in range(PIECES)]:
            for way in (1, -1):
                wires.wait(("r", way, 1, i), box(way, 1, i), near[-way])
            summed = part[rel(0), rows(i)] + (inbox[0, 0, rows(i)] + inbox[1, 0, rows(i)])
            value = weight[rows(i)] * (summed - target[rows(i)])
            total[rows(i)] = value
            for way in (1, -1):
                deliver(way, 0, i)
            residual[rel(0), rows(i)] = value

    def relay_residual(d, some=pairs, near_too=True):
        for way, i in some:
            if (d == 4 or not near_too) and not goes_far(way, i):
                continue
            wires.wait(("g", way, d - 1, i), residual.at[rel(-d * way), rows(i)], near[-way])
            if d < 3 or (d == 3 and goes_far(way, i)):
                deliver(way, d, i)

    def split_residual(k):
        place, number = CHUNKS[k]

        def one(j, _):
            for i in range(number):
                high, low = halves(residual[place + i, j])
                back[k][j, i * WIDTH : (i + 1) * WIDTH] = high
                back[k][j, length(k) + i * WIDTH : length(k) + (i + 1) * WIDTH] = low
            return 0

        lax.fori_loop(0, LIVE, one, 0, unroll=4)

    def start_grad(k):
        for dy in (2, 1, 3, 0):
            yy = turn(y, dy, NY)
            for n in range(NX * NC):
                at = within(lists[3, yy * (NX * NC) + n], n_tiles + 1)
                grad[yy, n // NC, n % NC, chunk(k)] = sums[at, 0 : length(k)]
            wires.send(("q", k, dy), grad.at[yy, :, 1 - core, chunk(k)], mine.at[yy, :, chunk(k)], partner)

    def spread_grad(k):
        for dy in (2, 1, 3, 0):
            yy = turn(y, dy, NY)
            wires.wait(("q", k, dy), mine.at[yy, :, chunk(k)], partner)
            for n, (to_y, dx) in enumerate(BY_ROW):
                if to_y == dy:
                    xx = turn(x, dx, NX)
                    mine[yy, xx, chunk(k)] += grad[yy, xx, core, chunk(k)]
                    wires.send(("t", k, n), mine.at[yy, xx, chunk(k)], terms.at[n, chunk(k)], peer(dy, dx))

    def finish_grad(k):
        value = mine[y, x, chunk(k)] + grad[y, x, core, chunk(k)]
        for n, (dy, dx) in enumerate(BY_ROW):
            wires.wait(("t", k, n), terms.at[n, chunk(k)], peer(-dy, -dx))
            value = value + terms[n, chunk(k)]
        place, number = CHUNKS[k]
        for i in range(number):
            out[0, slices_of(place + i)] = value[i * WIDTH : (i + 1) * WIDTH]

    quarter = n_tiles // 4
    for k in range(len(CHUNKS)):
        split_volume(k, rotated[chunk(k)], y, x, core)
        for j in range(LIVE, 32):
            back[k][j] = jnp.zeros(back[k].shape[1:], bf16)
    sums[0] = jnp.zeros(sums.shape[1:], f32)
    for b in range(batches):
        prepare(b)
    receive_volume(0)
    give.wait()
    receive_partner(0)
    forward(0, 0, n_tiles)
    take_part(0)
    start_sums()
    receive_volume(1)
    weigh()
    receive_partner(1)
    forward(1, 0, 2 * quarter)
    relay_sums(3, True)
    receive_volume(2)
    forward(1, 2 * quarter, 2 * quarter)
    take_part(1)
    relay_sums(2, False)
    receive_partner(2)
    forward(2, 0, quarter)
    relay_sums(2, True)
    forward(2, quarter, 3 * quarter)
    take_part(2)
    relay_sums(1, False)
    relay_sums(1, True)
    finish_sums()
    relay_residual(1)
    split_residual(2)
    backward(2, 0, quarter)
    relay_residual(2, pairs[0:2])
    relay_residual(2, pairs[2:4])
    backward(2, quarter, quarter)
    relay_residual(2, pairs[4:6])
    backward(2, 2 * quarter, 2 * quarter)
    relay_residual(2, pairs[6:8])
    start_grad(2)
    split_residual(1)
    relay_residual(3, pairs[0:4], near_too=False)
    backward(1, 0, 2 * quarter)
    spread_grad(2)
    backward(1, 2 * quarter, 2 * quarter)
    start_grad(1)
    relay_residual(3, pairs[4:8])
    relay_residual(4)
    split_residual(0)
    backward(0, 0, quarter)
    spread_grad(1)
    backward(0, quarter, 3 * quarter)
    start_grad(0)
    spread_grad(0)
    finish_grad(2)
    finish_grad(1)
    finish_grad(0)
    wires.drain()


def shards(volume, projector, tile_ids, counts, ray_counts):
    n_tiles, rays, lanes = projector.shape
    slices = volume.shape[1]
    n_sems = len(CHUNKS) * (3 * len(OFFSETS) + 1 + NY) + 4 * (PIECES // 2 + 3 * PIECES)
    lengths = [number * WIDTH for _, number in CHUNKS]
    gradient = pl.pallas_call(
        step_kernel,
        out_shape=jax.ShapeDtypeStruct(volume.shape, f32),
        in_specs=[VMEM, SMEM, VMEM, ANY, ANY],
        out_specs=VMEM,
        scratch_shapes=[
            pltpu.VMEM((slices, lanes), f32),
            pltpu.VMEM((NY, NX, NC, slices, lanes), f32),
            pltpu.VMEM((BUFFERS, BATCH, rays, lanes), f32),
            pltpu.VMEM((n_tiles, 2, rays, lanes), bf16),
            pltpu.VMEM((n_tiles, 2, lanes, rays), bf16),
            *[pltpu.VMEM((COLS, 2 * m, lanes), bf16) for m in lengths],
            *[pltpu.VMEM((32, 2 * m, rays), bf16) for m in lengths],
            pltpu.VMEM((n_tiles + 1, max(lengths), lanes), f32),
            pltpu.VMEM((NP, LIVE, WIDTH, rays), f32),
            pltpu.VMEM((2, 4, LIVE, WIDTH, rays), f32),
            pltpu.VMEM((LIVE, WIDTH, rays), f32),
            pltpu.VMEM((LIVE, WIDTH, rays), f32),
            pltpu.VMEM((NP, LIVE, WIDTH, rays), f32),
            pltpu.VMEM((LIVE, WIDTH, rays), f32),
            pltpu.VMEM((counts.shape[0], WIDTH, rays), i32),
            pltpu.VMEM((NY, NX, NC, slices, lanes), f32),
            pltpu.VMEM((NY, NX, slices, lanes), f32),
            pltpu.VMEM((len(OFFSETS), slices, lanes), f32),
            pltpu.VMEM((8, LANES), i32),
            pltpu.VMEM((8, LANES), i32),
            pltpu.SMEM((8, LANES), i32),
            pltpu.SemaphoreType.DMA((n_tiles // BATCH,)),
            pltpu.SemaphoreType.DMA((2,)),
            pltpu.SemaphoreType.DMA((n_sems,)),
            pltpu.SemaphoreType.DMA((n_sems,)),
        ],
        compiler_params=pltpu.CompilerParams(
            collective_id=0, has_side_effects=True, vmem_limit_bytes=62 << 20
        ),
        name="step",
    )(tile_ids.reshape(1, n_tiles), ray_counts, volume, projector, counts)
    return volume - STEP * gradient


def solution(mesh):
    placed = (
        P(("pix", "ang"), None, None),
        P(("pix", "ang"), None, None),
        P(("pix", "ang")),
        P("ang", None, None),
        P("ang", None),
    )
    return jax.shard_map(
        shards, mesh=mesh, in_specs=placed, out_specs=P(("pix", "ang"), None, None), check_vma=False
    )
```
